32 devices in a mesh: orb: 8 (over z, x), slab: 4 (over y, core).
Axes of the slice: x: 2, y: 2, z: 4, core: 2. Of those that a mesh axis runs over, the one named last changes fastest.
Arguments:
- orbitals: bfloat16 [8, 64, 64, 128], P('orb', 'slab'), may hold values from -6 to 6
- pair_table: int32 [64, 3], P('orb'), may hold values from -1 to 7, as said below
Outputs:
- exchange_action: float32 [8, 64, 64, 128], P('orb', 'slab')
The draws below stay inside these ranges and needn't reach their ends.
Inputs may be any that keep to these rules, and one draw needn't show every extreme that they name: `pair_table`: A live slot holds (m, n, s) with m <= n and s in 0, 1; an empty slot holds -1 in all three columns. A block of 8 slots has its live slots first. No (m, n, s) appears twice in the table. Exactly 36 slots are live, and the 8 blocks hold, in some order, k * 1 live slots for k = 1 to 8.
All inputs are finite; a program needn't handle non-finite values.
Results may differ from the reference program's by a relative error of at most 0.0003.
Values may be sent and summed in bfloat16 or wider, within the bound.
A program may use at most 64 MiB of HBM per device.

```python
import math
import jax
import jax.numpy as jnp
from jax import lax

G = 64
CP_DEV = 1
COUPLES = 8
N_ORB = 8


def draw_pair_table(key, part):
    couples = CP_DEV * N_ORB
    capacity = couples
    blocks = N_ORB
    upper_rows, upper_cols = jnp.triu_indices(couples)
    combos = upper_rows.shape[0] * 2
    shuffled = jax.random.permutation(jax.random.fold_in(key, 11), combos)
    ranking = jax.random.permutation(jax.random.fold_in(key, 12), blocks)
    counts = capacity * (ranking + 1) // blocks
    starts = jnp.cumsum(counts) - counts
    slot_index = jnp.arange(blocks * capacity, dtype=jnp.int32)
    block_of = slot_index // capacity
    column = slot_index % capacity
    is_live = column < counts[block_of]
    chosen = shuffled[jnp.where(is_live, starts[block_of] + column, 0)]
    pair_index = chosen // 2
    result_rows = jnp.stack([upper_rows[pair_index], upper_cols[pair_index], chosen % 2], axis=1).astype(jnp.int32)
    return jnp.where(is_live[:, None], result_rows, -1).astype(jnp.int32)


def steps_of(rng, extent, split, least, largest):
    level, own = 1.0, jax.random.fold_in(rng, 6)
    for dim, blocks in split:
        draws = jnp.exp(jax.random.uniform(jax.random.fold_in(own, dim), (blocks,), jnp.float32, least / len(split), largest / len(split)))
        level = level * jnp.repeat(draws, extent[dim] // blocks).reshape([-1 if axis == dim else 1 for axis in range(len(extent))])
    return level


def scatter_about(key, extent, deviation, bound, split=(), kind=jnp.bfloat16):
    gain = steps_of(key, extent, split, -0.22, 0.18) if split else 1.0
    array = jax.random.normal(key, extent, jnp.float32) * deviation * gain
    return jnp.minimum(jnp.maximum(array, -bound), bound).astype(kind)


def setup_inputs(seed: int = 0) -> dict:
    streams_of = jax.random.split(jax.random.key(seed), 3)
    orbitals = scatter_about(streams_of[0], (COUPLES, G, G, 2 * G), 1.0, 6.0, ((0, 8), (1, 4)))
    pair_table = draw_pair_table(jax.random.fold_in(streams_of[2], 71), 0)
    return dict(orbitals=orbitals, pair_table=pair_table)


exchange_fraction = 0.25
cell_ratio = 8.0


def folded(values, grid_len):
    return jnp.minimum(values, grid_len - values)


def kernel_half(grid_len):
    full_axis = folded(jnp.arange(grid_len, dtype=jnp.int32), grid_len).astype(jnp.float32)
    planes_x = cell_ratio * full_axis
    half_axis = jnp.arange(grid_len // 2 + 1, dtype=jnp.int32).astype(jnp.float32)
    scale_k = (2.0 * math.pi / grid_len) * (2.0 * math.pi / grid_len)
    squared = scale_k * (planes_x[:, None, None] * planes_x[:, None, None]
                         + full_axis[None, :, None] * full_axis[None, :, None]
                         + half_axis[None, None, :] * half_axis[None, None, :])
    safe_sq = jnp.where(squared > 0, squared, 1.0)
    return jnp.where(squared > 0, -exchange_fraction / safe_sq, 0.0)


def lane_swap(field_in, grid_len):
    return jnp.concatenate([field_in[..., grid_len:], field_in[..., :grid_len]], axis=-1)


def to_lanes(field_in, grid_len):
    return field_in.reshape(grid_len, grid_len, 2, grid_len).transpose(2, 0, 1, 3)


def from_lanes(field_in, grid_len):
    return field_in.transpose(1, 2, 0, 3).reshape(grid_len, grid_len, 2 * grid_len)


def reference(orbitals, pair_table):
    couples = orbitals.shape[0]
    grid_len = orbitals.shape[1]
    kernel = kernel_half(grid_len)

    def add_slot(totals, row_vals):
        first_id = row_vals[0]
        second_id = row_vals[1]
        left_rows = orbitals[first_id].astype(jnp.float32)
        right_rows = orbitals[second_id].astype(jnp.float32)
        partner = jnp.where(row_vals[2] == 1, lane_swap(right_rows, grid_len), right_rows)
        density = to_lanes(left_rows * partner, grid_len)
        spectrum = jnp.fft.rfftn(density, axes=(1, 2, 3))
        potential = jnp.fft.irfftn(spectrum * kernel[None], s=(grid_len, grid_len, grid_len), axes=(1, 2, 3))
        potential = from_lanes(potential.astype(left_rows.dtype), grid_len)
        first_term = potential * partner
        second_term = potential * left_rows
        second_term = jnp.where(row_vals[2] == 1, lane_swap(second_term, grid_len), second_term)
        totals = totals.at[first_id].add(first_term)
        return totals.at[second_id].add(jnp.where(first_id != second_id, second_term, 0.0))

    def visit(slot_index, totals):
        row_vals = pair_table[slot_index]
        return lax.cond(row_vals[0] >= 0, lambda acc_in: add_slot(acc_in, row_vals), lambda acc_in: acc_in, totals)

    totals = lax.fori_loop(0, pair_table.shape[0], visit, jnp.zeros(orbitals.shape, jnp.float32))
    orbital_count = 2 * couples
    cell_count = grid_len * grid_len * grid_len
    orbital_grid = orbitals.astype(jnp.float32).reshape(couples, grid_len, grid_len, 2, grid_len)
    orbital_grid = orbital_grid.transpose(0, 3, 1, 2, 4).reshape(orbital_count, cell_count)
    actions = totals.reshape(couples, grid_len, grid_len, 2, grid_len)
    actions = actions.transpose(0, 3, 1, 2, 4).reshape(orbital_count, cell_count)
    intersection = lax.dot_general(orbital_grid, actions, (((1,), (1,)), ((), ())), precision=lax.Precision.HIGHEST) / cell_count
    corrected = actions - lax.dot_general(intersection, orbital_grid, (((0,), (0,)), ((), ())), precision=lax.Precision.HIGHEST)
    corrected = corrected.reshape(couples, 2, grid_len, grid_len, grid_len).transpose(0, 2, 3, 1, 4)
    return corrected.reshape(orbitals.shape)
```

```python
import functools
import math

import jax
import jax.numpy as jnp
import numpy as np
from jax import lax
from jax.experimental import pallas as pl
from jax.experimental.pallas import tpu as pltpu
from jax.sharding import PartitionSpec as P

exchange_fraction = 0.25
cell_ratio = 8.0
MESH = pl.DeviceIdType.MESH
VMEM_SPEC = pl.BlockSpec(memory_space=pltpu.VMEM)
ANY_SPEC = pl.BlockSpec(memory_space=pl.ANY)


def folded(values, grid_len):
    return jnp.minimum(values, grid_len - values).astype(jnp.float32)


def hartley(grid_len):
    rows_idx = np.arange(grid_len)
    angles = 2.0 * math.pi / grid_len * (rows_idx[:, None] * rows_idx[None, :] % grid_len)
    return ((np.cos(angles) + np.sin(angles)) / math.sqrt(grid_len)).astype(np.float32)


def split_const(values):
    high = values.astype(jnp.bfloat16)
    return high, (values - high.astype(np.float32)).astype(jnp.bfloat16)


def split(values):
    high = values.astype(jnp.bfloat16)
    low = (values - high.astype(jnp.float32)).astype(jnp.bfloat16)
    return high, low


def coulomb(grid_len, slab_len, slab_index):
    planes_x = cell_ratio * folded(jnp.arange(grid_len, dtype=jnp.int32), grid_len)
    rows_y = folded(slab_index * slab_len + jnp.arange(slab_len, dtype=jnp.int32), grid_len)
    depth_z = folded(jnp.arange(2 * grid_len, dtype=jnp.int32) % grid_len, grid_len)
    scale_k = 2.0 * math.pi / grid_len * (2.0 * math.pi / grid_len)
    squared = scale_k * (
        planes_x[:, None, None] * planes_x[:, None, None]
        + rows_y[None, :, None] * rows_y[None, :, None]
        + depth_z[None, None, :] * depth_z[None, None, :]
    )
    safe_sq = jnp.where(squared > 0, squared, 1.0)
    return jnp.where(squared > 0, -exchange_fraction / safe_sq, 0.0)


def axis_parts(count):
    inner = 1
    while inner * inner * 4 <= count and count % (inner * 2) == 0:
        inner *= 2
    return count // inner, inner


def peer(index):
    return {"orb": index}


def greet_all(count, me):
    barrier = pltpu.get_barrier_semaphore()
    for step in range(1, count):
        pl.semaphore_signal(
            barrier, inc=1, device_id=peer(lax.rem(me + step, count)), device_id_type=MESH
        )
    pl.semaphore_wait(barrier, count - 1)


def gather_kernel(count, own_ref, table_ref, out_ref, tables_ref, local_sem, up_send, up_recv,
                  down_send, down_recv, side_send, side_recv, tab_send, tab_recv):
    outer, inner = axis_parts(count)
    me = lax.axis_index("orb")
    z_pos, x_pos = me // inner, me % inner
    greet_all(count, me)

    def slot(z_at, x_at):
        return out_ref.at[z_at * inner + x_at]

    def up_copy(step, src):
        return pltpu.make_async_remote_copy(
            src_ref=src, dst_ref=slot(z_pos - step, x_pos), send_sem=up_send.at[step],
            recv_sem=up_recv.at[step], device_id=peer((z_pos + 1) * inner + x_pos),
            device_id_type=MESH)

    def down_copy(step, src):
        return pltpu.make_async_remote_copy(
            src_ref=src, dst_ref=slot(z_pos + step, x_pos), send_sem=down_send.at[step],
            recv_sem=down_recv.at[step], device_id=peer((z_pos - 1) * inner + x_pos),
            device_id_type=MESH)

    def side_copy(hop, z_at, src):
        return pltpu.make_async_remote_copy(
            src_ref=src, dst_ref=slot(z_at, x_pos), send_sem=side_send.at[hop - 1, z_at],
            recv_sem=side_recv.at[hop - 1, z_at],
            device_id=peer(z_pos * inner + lax.rem(x_pos + hop, inner)), device_id_type=MESH)

    def tab_copy(step):
        return pltpu.make_async_remote_copy(
            src_ref=table_ref, dst_ref=tables_ref.at[me], send_sem=tab_send.at[step - 1],
            recv_sem=tab_recv.at[step - 1], device_id=peer(lax.rem(me + step, count)),
            device_id_type=MESH)

    has_up, has_down = z_pos + 1 < outer, z_pos >= 1

    @pl.when(has_up)
    def _():
        up_copy(0, own_ref).start()

    @pl.when(has_down)
    def _():
        down_copy(0, own_ref).start()

    for hop in range(1, inner):
        side_copy(hop, z_pos, own_ref).start()
    for step in range(1, count):
        tab_copy(step).start()
    keep = pltpu.make_async_copy(own_ref, out_ref.at[me], local_sem.at[0])
    keep.start()
    keep_tab = pltpu.make_async_copy(table_ref, tables_ref.at[me], local_sem.at[1])
    keep_tab.start()

    for step in range(1, outer):
        @pl.when(z_pos - step >= 0)
        def _():
            held = slot(z_pos - step, x_pos)
            up_copy(step - 1, held).wait_recv()

            @pl.when(has_up)
            def _():
                up_copy(step, held).start()

            for hop in range(1, inner):
                side_copy(hop, z_pos - step, held).start()

        @pl.when(z_pos + step < outer)
        def _():
            held = slot(z_pos + step, x_pos)
            down_copy(step - 1, held).wait_recv()

            @pl.when(has_down)
            def _():
                down_copy(step, held).start()

            for hop in range(1, inner):
                side_copy(hop, z_pos + step, held).start()

    keep.wait()
    keep_tab.wait()
    for hop in range(1, inner):
        for z_at in range(outer):
            side_copy(hop, z_at, own_ref).wait_recv()
            side_copy(hop, z_at, own_ref).wait_send()
    for step in range(1, count):
        tab_copy(step).wait_recv()
        tab_copy(step).wait_send()
    for step in range(outer):
        @pl.when(has_up & (z_pos - step >= 0))
        def _():
            up_copy(step, own_ref).wait_send()

        @pl.when(has_down & (z_pos + step < outer))
        def _():
            down_copy(step, own_ref).wait_send()


def gather_all(own, table, count):
    outer, inner = axis_parts(count)
    dma = pltpu.SemaphoreType.DMA
    return pl.pallas_call(
        functools.partial(gather_kernel, count),
        out_shape=(
            jax.ShapeDtypeStruct((count,) + own.shape, own.dtype),
            jax.ShapeDtypeStruct((count,) + table.shape, table.dtype),
        ),
        in_specs=[VMEM_SPEC, VMEM_SPEC],
        out_specs=(ANY_SPEC, ANY_SPEC),
        scratch_shapes=[dma((2,)), dma((outer,)), dma((outer,)), dma((outer,)), dma((outer,)),
                        dma((max(inner - 1, 1), outer)), dma((max(inner - 1, 1), outer)),
                        dma((count - 1,)), dma((count - 1,))],
        compiler_params=pltpu.CompilerParams(collective_id=0, has_side_effects=True),
    )(own, table)


def scatter_kernel(count, parts_ref, out_ref, side_in, line_in, sums, own_sem, side_send,
                   side_recv, line_send, line_recv):
    outer, inner = axis_parts(count)
    me = lax.axis_index("orb")
    z_pos, x_pos = me // inner, me % inner
    greet_all(count, me)

    def side_copy(hop, turn):
        z_at = lax.rem(z_pos + turn, outer)
        x_to = lax.rem(x_pos + hop, inner)
        return pltpu.make_async_remote_copy(
            src_ref=parts_ref.at[z_at * inner + x_to], dst_ref=side_in.at[hop - 1, turn],
            send_sem=side_send.at[hop - 1, turn], recv_sem=side_recv.at[hop - 1, turn],
            device_id=peer(z_pos * inner + x_to), device_id_type=MESH)

    def line_copy(turn):
        z_at = lax.rem(z_pos + turn, outer)
        return pltpu.make_async_remote_copy(
            src_ref=sums.at[turn], dst_ref=line_in.at[turn - 1],
            send_sem=line_send.at[turn - 1], recv_sem=line_recv.at[turn - 1],
            device_id=peer(z_at * inner + x_pos), device_id_type=MESH)

    def own_copy(turn):
        z_at = lax.rem(z_pos + turn, outer)
        return pltpu.make_async_copy(
            parts_ref.at[z_at * inner + x_pos], sums.at[turn], own_sem.at[turn])

    order = list(range(1, outer)) + [0]
    for turn in order:
        for hop in range(1, inner):
            side_copy(hop, turn).start()
        own_copy(turn).start()
    for turn in order:
        own_copy(turn).wait()
        for hop in range(1, inner):
            side_copy(hop, turn).wait_recv()
            sums[turn] = sums[turn] + side_in[hop - 1, turn]
        if turn:
            line_copy(turn).start()
    total = sums[0]
    for turn in range(1, outer):
        line_copy(turn).wait_recv()
        total = total + line_in[turn - 1]
    out_ref[...] = total
    for turn in range(outer):
        for hop in range(1, inner):
            side_copy(hop, turn).wait_send()
        if turn:
            line_copy(turn).wait_send()


def scatter_sum(parts, count):
    outer, inner = axis_parts(count)
    dma = pltpu.SemaphoreType.DMA
    block = parts.shape[1:]
    sides, lines = max(inner - 1, 1), max(outer - 1, 1)
    return pl.pallas_call(
        functools.partial(scatter_kernel, count),
        out_shape=jax.ShapeDtypeStruct(block, parts.dtype),
        in_specs=[ANY_SPEC],
        out_specs=VMEM_SPEC,
        scratch_shapes=[
            pltpu.VMEM((sides, outer) + block, parts.dtype),
            pltpu.VMEM((lines,) + block, parts.dtype),
            pltpu.VMEM((outer,) + block, parts.dtype),
            dma((outer,)), dma((sides, outer)), dma((sides, outer)), dma((lines,)), dma((lines,)),
        ],
        compiler_params=pltpu.CompilerParams(collective_id=1, has_side_effects=True),
    )(parts)


def depth_turn(rows, depth_ref):
    width = rows.shape[1]
    high, low = split(rows)
    both = jnp.dot(jnp.concatenate([high, low], axis=1), depth_ref[...],
                   preferred_element_type=jnp.float32)
    return both[:, :width] + both[:, width:]


def pair_turn(first, second, left_ref):
    high, low = split(jnp.concatenate([first, second], axis=1))
    return jnp.dot(left_ref[...], jnp.concatenate([high, low, high], axis=0),
                   preferred_element_type=jnp.float32)


def forward_kernel(grid_len, ids_ref, left_ref, right_ref, depth_ref, turn_ref, out_ref):
    step = pl.program_id(0)
    left = left_ref[0].astype(jnp.float32)
    right = right_ref[0].astype(jnp.float32)
    width = right.shape[1]
    partner = jnp.where(ids_ref[step, 2] == 1, pltpu.roll(right, grid_len, 1), right)
    density = jnp.where(ids_ref[step, 3] == 1, left * partner, 0.0)
    flat = depth_turn(density, depth_ref)
    for x_at in range(0, flat.shape[0] // grid_len, 2):
        low, mid, high = x_at * grid_len, (x_at + 1) * grid_len, (x_at + 2) * grid_len
        done = pair_turn(flat[low:mid], flat[mid:high], turn_ref)
        out_ref[0, low:mid] = done[:, :width]
        out_ref[0, mid:high] = done[:, width:]


def middle_kernel(grid_len, slab_len, in_ref, kernel_ref, turn_ref, out_ref):
    width = in_ref.shape[2]
    for row in range(0, slab_len, 2):
        one = pl.ds(row, grid_len, stride=slab_len)
        two = pl.ds(row + 1, grid_len, stride=slab_len)
        done = pair_turn(in_ref[0, one, :], in_ref[0, two, :], turn_ref)
        back = pair_turn(done[:, :width] * kernel_ref[one, :], done[:, width:] * kernel_ref[two, :],
                         turn_ref)
        out_ref[0, one, :] = back[:, :width]
        out_ref[0, two, :] = back[:, width:]


def backward_kernel(grid_len, ids_ref, in_ref, left_ref, right_ref, depth_ref, turn_ref, out_ref,
                    flat_ref):
    step = pl.program_id(0)

    @pl.when(step == 0)
    def _():
        out_ref[...] = jnp.zeros_like(out_ref)

    width = flat_ref.shape[1]
    for x_at in range(0, flat_ref.shape[0] // grid_len, 2):
        low, mid, high = x_at * grid_len, (x_at + 1) * grid_len, (x_at + 2) * grid_len
        done = pair_turn(in_ref[0, low:mid], in_ref[0, mid:high], turn_ref)
        flat_ref[low:mid] = done[:, :width]
        flat_ref[mid:high] = done[:, width:]
    potential = depth_turn(flat_ref[...], depth_ref)
    first_id, second_id = ids_ref[step, 0], ids_ref[step, 1]
    flipped = ids_ref[step, 2] == 1
    is_used = ids_ref[step, 3] == 1

    @pl.when(is_used)
    def _():
        right = right_ref[0].astype(jnp.float32)
        partner = jnp.where(flipped, pltpu.roll(right, grid_len, 1), right)
        out_ref[first_id] += potential * partner

    @pl.when(is_used & (first_id != second_id))
    def _():
        second = potential * left_ref[0].astype(jnp.float32)
        out_ref[second_id] += jnp.where(flipped, pltpu.roll(second, grid_len, 1), second)


def local(orbitals, pair_table, n_orb):
    couples_own, slab_len, grid_len, width = orbitals.shape
    rows = slab_len * grid_len
    capacity = pair_table.shape[0]
    couples = couples_own * n_orb
    padded = jnp.pad(pair_table, ((0, 0), (0, 128 - pair_table.shape[1])), constant_values=-1)
    gathered, tables = gather_all(orbitals.reshape(couples_own * rows, width), padded, n_orb)
    gathered = gathered.reshape(couples, rows, width)
    table = tables.reshape(n_orb * capacity, 128)[:, :3]

    live_total = sum(capacity * (k + 1) // n_orb for k in range(n_orb))
    per_device = -(-live_total // n_orb)
    is_live = table[:, 0] >= 0
    rank = jnp.cumsum(is_live.astype(jnp.int32)) - 1
    wanted = jnp.arange(per_device, dtype=jnp.int32) * n_orb + lax.axis_index("orb")
    hits = (rank[None, :] == wanted[:, None]) & is_live[None, :]
    picked = jnp.sum(jnp.where(hits[:, :, None], table[None], 0), axis=1)
    used = jnp.any(hits, axis=1).astype(jnp.int32)
    ids = jnp.concatenate([picked, used[:, None]], axis=1)

    mat = hartley(grid_len)
    mat_high, mat_low = split_const(mat)
    turn_mat = jnp.asarray(np.concatenate([mat_high, mat_high, mat_low], axis=1))
    deep_high, deep_low = split_const(np.kron(np.eye(2, dtype=np.float32), mat))
    depth_mat = jnp.asarray(np.block([[deep_high, deep_low],
                                      [deep_high, np.zeros_like(deep_low)]]))
    kernel = coulomb(grid_len, slab_len, lax.axis_index("slab")).reshape(grid_len * slab_len, width)

    def whole(shape):
        return pl.BlockSpec(shape, lambda j, *ids: (0,) * len(shape))

    left_spec = pl.BlockSpec((1, rows, width), lambda j, ids: (ids[j, 0], 0, 0))
    right_spec = pl.BlockSpec((1, rows, width), lambda j, ids: (ids[j, 1], 0, 0))
    slot_spec = pl.BlockSpec((1, rows, width), lambda j, *ids: (j, 0, 0))
    slots_shape = jax.ShapeDtypeStruct((per_device, rows, width), jnp.float32)

    spectra = pl.pallas_call(
        functools.partial(forward_kernel, grid_len),
        out_shape=slots_shape,
        grid_spec=pltpu.PrefetchScalarGridSpec(
            num_scalar_prefetch=1, grid=(per_device,),
            in_specs=[left_spec, right_spec, whole(depth_mat.shape), whole(turn_mat.shape)],
            out_specs=slot_spec),
    )(ids, gathered, gathered, depth_mat, turn_mat)
    crossed = lax.all_to_all(spectra.reshape(per_device, slab_len, grid_len, width), "slab",
                             split_axis=2, concat_axis=1, tiled=True)
    solved = pl.pallas_call(
        functools.partial(middle_kernel, grid_len, slab_len),
        out_shape=slots_shape,
        grid=(per_device,),
        in_specs=[slot_spec, whole(kernel.shape), whole(turn_mat.shape)],
        out_specs=slot_spec,
    )(crossed.reshape(per_device, rows, width), kernel, turn_mat)
    returned = lax.all_to_all(solved.reshape(per_device, grid_len, slab_len, width), "slab",
                              split_axis=1, concat_axis=2, tiled=True)
    totals = pl.pallas_call(
        functools.partial(backward_kernel, grid_len),
        out_shape=jax.ShapeDtypeStruct((couples, rows, width), jnp.float32),
        grid_spec=pltpu.PrefetchScalarGridSpec(
            num_scalar_prefetch=1, grid=(per_device,),
            in_specs=[slot_spec, left_spec, right_spec, whole(depth_mat.shape),
                      whole(turn_mat.shape)],
            out_specs=whole((couples, rows, width)),
            scratch_shapes=[pltpu.VMEM((rows, width), jnp.float32)]),
    )(ids, returned.reshape(per_device, rows, width), gathered, gathered, depth_mat, turn_mat)

    own = scatter_sum(totals.reshape(n_orb, couples_own * rows, width), n_orb)
    own = own.reshape(couples_own, rows, width)
    cell_count = grid_len * grid_len * grid_len

    def swap(values):
        return jnp.concatenate([values[..., grid_len:], values[..., :grid_len]], axis=-1)

    def lanes(values):
        summed = values.reshape(values.shape[:-1] + (2, grid_len)).sum(axis=-1)
        return jnp.repeat(summed, grid_len, axis=-1)

    basis = gathered.astype(jnp.float32)
    turned = swap(own)
    straight = jnp.sum(basis[None] * own[:, None], axis=2)
    across = jnp.sum(basis[None] * turned[:, None], axis=2)
    both = lax.psum(lanes(jnp.stack([straight, across])) / cell_count, "slab")
    kept = jnp.sum(both[0][:, :, None, :] * basis[None], axis=1)
    moved = jnp.sum(both[1][:, :, None, :] * basis[None], axis=1)
    return (own - kept - swap(moved)).reshape(orbitals.shape)


def solution(mesh):
    placed = (P("orb", "slab", None, None), P("orb", None))
    return jax.shard_map(
        functools.partial(local, n_orb=mesh.shape["orb"]),
        mesh=mesh, in_specs=placed, out_specs=P("orb", "slab", None, None), check_vma=False
    )
```

```python
import functools
import math

import jax
import jax.numpy as jnp
import numpy as np
from jax import lax
from jax.experimental import pallas as pl
from jax.experimental.pallas import tpu as pltpu
from jax.sharding import PartitionSpec as P

exchange_fraction = 0.25
cell_ratio = 8.0
MESH = pl.DeviceIdType.MESH
VMEM_SPEC = pl.BlockSpec(memory_space=pltpu.VMEM)
ANY_SPEC = pl.BlockSpec(memory_space=pl.ANY)


def folded(values, grid_len):
    return jnp.minimum(values, grid_len - values).astype(jnp.float32)


def hartley(grid_len):
    rows_idx = np.arange(grid_len)
    angles = 2.0 * math.pi / grid_len * (rows_idx[:, None] * rows_idx[None, :] % grid_len)
    return ((np.cos(angles) + np.sin(angles)) / math.sqrt(grid_len)).astype(np.float32)


def split_const(values):
    high = values.astype(jnp.bfloat16)
    return high, (values - high.astype(np.float32)).astype(jnp.bfloat16)


def split(values):
    high = values.astype(jnp.bfloat16)
    low = (values - high.astype(jnp.float32)).astype(jnp.bfloat16)
    return high, low


def coulomb(grid_len, slab_len, slab_index):
    planes_x = cell_ratio * folded(jnp.arange(grid_len, dtype=jnp.int32), grid_len)
    rows_y = folded(slab_index * slab_len + jnp.arange(slab_len, dtype=jnp.int32), grid_len)
    depth_z = folded(jnp.arange(2 * grid_len, dtype=jnp.int32) % grid_len, grid_len)
    scale_k = 2.0 * math.pi / grid_len * (2.0 * math.pi / grid_len)
    squared = scale_k * (
        planes_x[:, None, None] * planes_x[:, None, None]
        + rows_y[None, :, None] * rows_y[None, :, None]
        + depth_z[None, None, :] * depth_z[None, None, :]
    )
    safe_sq = jnp.where(squared > 0, squared, 1.0)
    return jnp.where(squared > 0, -exchange_fraction / safe_sq, 0.0)


def axis_parts(count):
    inner = 1
    while inner * inner * 4 <= count and count % (inner * 2) == 0:
        inner *= 2
    return count // inner, inner


def peer(index):
    return {"orb": index}


def greet_all(count, me):
    barrier = pltpu.get_barrier_semaphore()
    for step in range(1, count):
        pl.semaphore_signal(
            barrier, inc=1, device_id=peer(lax.rem(me + step, count)), device_id_type=MESH
        )
    pl.semaphore_wait(barrier, count - 1)


def gather_kernel(count, own_ref, table_ref, out_ref, tables_ref, local_sem, up_send, up_recv,
                  down_send, down_recv, side_send, side_recv, tab_send, tab_recv):
    outer, inner = axis_parts(count)
    me = lax.axis_index("orb")
    z_pos, x_pos = me // inner, me % inner
    greet_all(count, me)

    def slot(z_at, x_at):
        return out_ref.at[z_at * inner + x_at]

    def up_copy(step, src):
        return pltpu.make_async_remote_copy(
            src_ref=src, dst_ref=slot(z_pos - step, x_pos), send_sem=up_send.at[step],
            recv_sem=up_recv.at[step], device_id=peer((z_pos + 1) * inner + x_pos),
            device_id_type=MESH)

    def down_copy(step, src):
        return pltpu.make_async_remote_copy(
            src_ref=src, dst_ref=slot(z_pos + step, x_pos), send_sem=down_send.at[step],
            recv_sem=down_recv.at[step], device_id=peer((z_pos - 1) * inner + x_pos),
            device_id_type=MESH)

    def side_copy(hop, z_at, src):
        return pltpu.make_async_remote_copy(
            src_ref=src, dst_ref=slot(z_at, x_pos), send_sem=side_send.at[hop - 1, z_at],
            recv_sem=side_recv.at[hop - 1, z_at],
            device_id=peer(z_pos * inner + lax.rem(x_pos + hop, inner)), device_id_type=MESH)

    def tab_copy(step):
        return pltpu.make_async_remote_copy(
            src_ref=table_ref, dst_ref=tables_ref.at[me], send_sem=tab_send.at[step - 1],
            recv_sem=tab_recv.at[step - 1], device_id=peer(lax.rem(me + step, count)),
            device_id_type=MESH)

    has_up, has_down = z_pos + 1 < outer, z_pos >= 1

    @pl.when(has_up)
    def _():
        up_copy(0, own_ref).start()

    @pl.when(has_down)
    def _():
        down_copy(0, own_ref).start()

    for hop in range(1, inner):
        side_copy(hop, z_pos, own_ref).start()
    for step in range(1, count):
        tab_copy(step).start()
    keep = pltpu.make_async_copy(own_ref, out_ref.at[me], local_sem.at[0])
    keep.start()
    keep_tab = pltpu.make_async_copy(table_ref, tables_ref.at[me], local_sem.at[1])
    keep_tab.start()

    for step in range(1, outer):
        @pl.when(z_pos - step >= 0)
        def _():
            held = slot(z_pos - step, x_pos)
            up_copy(step - 1, held).wait_recv()

            @pl.when(has_up)
            def _():
                up_copy(step, held).start()

            for hop in range(1, inner):
                side_copy(hop, z_pos - step, held).start()

        @pl.when(z_pos + step < outer)
        def _():
            held = slot(z_pos + step, x_pos)
            down_copy(step - 1, held).wait_recv()

            @pl.when(has_down)
            def _():
                down_copy(step, held).start()

            for hop in range(1, inner):
                side_copy(hop, z_pos + step, held).start()

    keep.wait()
    keep_tab.wait()
    for hop in range(1, inner):
        for z_at in range(outer):
            side_copy(hop, z_at, own_ref).wait_recv()
            side_copy(hop, z_at, own_ref).wait_send()
    for step in range(1, count):
        tab_copy(step).wait_recv()
        tab_copy(step).wait_send()
    for step in range(outer):
        @pl.when(has_up & (z_pos - step >= 0))
        def _():
            up_copy(step, own_ref).wait_send()

        @pl.when(has_down & (z_pos + step < outer))
        def _():
            down_copy(step, own_ref).wait_send()


def gather_all(own, table, count):
    outer, inner = axis_parts(count)
    dma = pltpu.SemaphoreType.DMA
    return pl.pallas_call(
        functools.partial(gather_kernel, count),
        out_shape=(
            jax.ShapeDtypeStruct((count,) + own.shape, own.dtype),
            jax.ShapeDtypeStruct((count,) + table.shape, table.dtype),
        ),
        in_specs=[VMEM_SPEC, VMEM_SPEC],
        out_specs=(ANY_SPEC, ANY_SPEC),
        scratch_shapes=[dma((2,)), dma((outer,)), dma((outer,)), dma((outer,)), dma((outer,)),
                        dma((max(inner - 1, 1), outer)), dma((max(inner - 1, 1), outer)),
                        dma((count - 1,)), dma((count - 1,))],
        compiler_params=pltpu.CompilerParams(collective_id=0, has_side_effects=True),
    )(own, table)


def depth_turn(rows, depth_ref):
    width = rows.shape[1]
    high, low = split(rows)
    both = jnp.dot(jnp.concatenate([high, low], axis=1), depth_ref[...],
                   preferred_element_type=jnp.float32)
    return both[:, :width] + both[:, width:]


def pair_turn(first, second, left_ref):
    high, low = split(jnp.concatenate([first, second], axis=1))
    return jnp.dot(left_ref[...], jnp.concatenate([high, low, high], axis=0),
                   preferred_element_type=jnp.float32)


def forward_kernel(grid_len, ids_ref, left_ref, right_ref, depth_ref, turn_ref, out_ref):
    step = pl.program_id(0)
    left = left_ref[0].astype(jnp.float32)
    right = right_ref[0].astype(jnp.float32)
    width = right.shape[1]
    partner = jnp.where(ids_ref[step, 2] == 1, pltpu.roll(right, grid_len, 1), right)
    density = jnp.where(ids_ref[step, 3] == 1, left * partner, 0.0)
    flat = depth_turn(density, depth_ref)
    for x_at in range(0, flat.shape[0] // grid_len, 2):
        low, mid, high = x_at * grid_len, (x_at + 1) * grid_len, (x_at + 2) * grid_len
        done = pair_turn(flat[low:mid], flat[mid:high], turn_ref)
        out_ref[0, low:mid] = done[:, :width]
        out_ref[0, mid:high] = done[:, width:]


def middle_kernel(grid_len, slab_len, in_ref, kernel_ref, turn_ref, out_ref):
    width = in_ref.shape[2]
    for row in range(0, slab_len, 2):
        one = pl.ds(row, grid_len, stride=slab_len)
        two = pl.ds(row + 1, grid_len, stride=slab_len)
        done = pair_turn(in_ref[0, one, :], in_ref[0, two, :], turn_ref)
        back = pair_turn(done[:, :width] * kernel_ref[one, :], done[:, width:] * kernel_ref[two, :],
                         turn_ref)
        out_ref[0, one, :] = back[:, :width]
        out_ref[0, two, :] = back[:, width:]


def return_kernel(n_orb, n_slab, chunks, couples_own, ids_ref, weights_ref, solved_ref, basis_ref,
                  depth_ref, turn_ref, out_ref, back, terms, flat_ref, parts, side_in, line_in, sums,
                  keep_sem, back_send, back_recv, side_send, side_recv, line_send, line_recv):
    outer, inner = axis_parts(n_orb)
    me, me_slab = lax.axis_index("orb"), lax.axis_index("slab")
    z_pos, x_pos = me // inner, me % inner
    slots, grid_len, slab_len, width = solved_ref.shape
    planes = slab_len // chunks
    rows = planes * grid_len

    barrier = pltpu.get_barrier_semaphore()
    for step in range(1, n_orb):
        pl.semaphore_signal(barrier, inc=1, device_id=peer(lax.rem(me + step, n_orb)),
                            device_id_type=MESH)
    for step in range(1, n_slab):
        pl.semaphore_signal(barrier, inc=1, device_id={"slab": lax.rem(me_slab + step, n_slab)},
                            device_id_type=MESH)
    pl.semaphore_wait(barrier, n_orb + n_slab - 2)

    own_rows = pl.ds(pl.multiple_of(me_slab * slab_len, slab_len), slab_len)

    def back_copy(chunk, hop):
        to = lax.rem(me_slab + hop, n_slab)
        return pltpu.make_async_remote_copy(
            src_ref=solved_ref.at[:, pl.ds(to * slab_len + chunk * planes, planes)],
            dst_ref=back.at[chunk, :, :, own_rows],
            send_sem=back_send.at[chunk, hop - 1], recv_sem=back_recv.at[chunk, hop - 1],
            device_id={"slab": to}, device_id_type=MESH)

    def keep_copy(chunk):
        return pltpu.make_async_copy(
            solved_ref.at[:, pl.ds(me_slab * slab_len + chunk * planes, planes)],
            back.at[chunk, :, :, own_rows], keep_sem.at[chunk])

    def side_copy(chunk, hop, turn):
        z_at = lax.rem(z_pos + turn, outer)
        x_to = lax.rem(x_pos + hop, inner)
        return pltpu.make_async_remote_copy(
            src_ref=parts.at[chunk, z_at * inner + x_to], dst_ref=side_in.at[chunk, hop - 1, turn],
            send_sem=side_send.at[chunk, hop - 1, turn], recv_sem=side_recv.at[chunk, hop - 1, turn],
            device_id=peer(z_pos * inner + x_to), device_id_type=MESH)

    def line_copy(chunk, turn):
        z_at = lax.rem(z_pos + turn, outer)
        return pltpu.make_async_remote_copy(
            src_ref=sums.at[chunk, turn], dst_ref=line_in.at[chunk, turn - 1],
            send_sem=line_send.at[chunk, turn - 1], recv_sem=line_recv.at[chunk, turn - 1],
            device_id=peer(z_at * inner + x_pos), device_id_type=MESH)

    order = list(range(1, outer)) + [0]

    def compute(chunk):
        keep_copy(chunk).wait()
        for hop in range(1, n_slab):
            back_copy(chunk, hop).wait_recv()

        @pl.loop(0, slots)
        def _(slot):
            for x_at in range(0, planes, 2):
                done = pair_turn(back[chunk, slot, x_at], back[chunk, slot, x_at + 1], turn_ref)
                flat_ref[x_at * grid_len:(x_at + 1) * grid_len] = done[:, :width]
                flat_ref[(x_at + 1) * grid_len:(x_at + 2) * grid_len] = done[:, width:]
            potential = depth_turn(flat_ref[...], depth_ref)
            flipped = ids_ref[slot, 2] == 1
            span = pl.ds(chunk * rows, rows)
            right = basis_ref[ids_ref[slot, 1], span].astype(jnp.float32)
            left = basis_ref[ids_ref[slot, 0], span].astype(jnp.float32)
            terms[2 * slot] = potential * jnp.where(flipped, pltpu.roll(right, grid_len, 1), right)
            second = potential * left
            terms[2 * slot + 1] = jnp.where(flipped, pltpu.roll(second, grid_len, 1), second)

        tile = 32

        @pl.loop(0, rows // tile)
        def _(at):
            here = pl.ds(pl.multiple_of(at * tile, tile), tile)

            @pl.loop(0, n_orb)
            def _(owner):
                for k in range(couples_own):
                    total = jnp.zeros((tile, width), jnp.float32)
                    for term in range(2 * slots):
                        total += weights_ref[owner * couples_own + k, term] * terms[term, here]
                    parts[chunk, owner, k, here] = total

        for turn in order:
            for hop in range(1, inner):
                side_copy(chunk, hop, turn).start()

    def forward(chunk):
        for turn in order:
            merged = parts[chunk, lax.rem(z_pos + turn, outer) * inner + x_pos]
            for hop in range(1, inner):
                side_copy(chunk, hop, turn).wait_recv()
                merged = merged + side_in[chunk, hop - 1, turn]
            sums[chunk, turn] = merged
            if turn:
                line_copy(chunk, turn).start()

    for chunk in range(chunks):
        for hop in range(1, n_slab):
            back_copy(chunk, hop).start()
        keep_copy(chunk).start()
    for chunk in range(chunks):
        compute(chunk)
        if chunk:
            forward(chunk - 1)
    forward(chunks - 1)
    for chunk in range(chunks):
        total = sums[chunk, 0]
        for turn in range(1, outer):
            line_copy(chunk, turn).wait_recv()
            total = total + line_in[chunk, turn - 1]
        out_ref[:, chunk * rows:(chunk + 1) * rows] = total
    for chunk in range(chunks):
        for hop in range(1, n_slab):
            back_copy(chunk, hop).wait_send()
        for turn in range(outer):
            for hop in range(1, inner):
                side_copy(chunk, hop, turn).wait_send()
            if turn:
                line_copy(chunk, turn).wait_send()


def return_sum(ids, weights, solved, basis, depth_mat, turn_mat, n_orb, n_slab):
    outer, inner = axis_parts(n_orb)
    slots, grid_len, slab_len, width = solved.shape
    couples_own = basis.shape[0] // n_orb
    chunks = max(1, min(4, slab_len // 2))
    planes = slab_len // chunks
    rows = planes * grid_len
    sides, lines = max(inner - 1, 1), max(outer - 1, 1)
    dma, vmem, f32 = pltpu.SemaphoreType.DMA, pltpu.VMEM, jnp.float32
    smem = pl.BlockSpec(memory_space=pltpu.SMEM)
    block = (couples_own, rows, width)
    return pl.pallas_call(
        functools.partial(return_kernel, n_orb, n_slab, chunks, couples_own),
        out_shape=jax.ShapeDtypeStruct((couples_own, slab_len * grid_len, width), f32),
        in_specs=[smem, smem] + [VMEM_SPEC] * 4,
        out_specs=VMEM_SPEC,
        scratch_shapes=[
            vmem((chunks, slots, planes, grid_len, width), f32),
            vmem((2 * slots, rows, width), f32),
            vmem((rows, width), f32),
            vmem((chunks, n_orb) + block, f32),
            vmem((chunks, sides, outer) + block, f32),
            vmem((chunks, lines) + block, f32),
            vmem((chunks, outer) + block, f32),
            dma((chunks,)),
            dma((chunks, max(n_slab - 1, 1))), dma((chunks, max(n_slab - 1, 1))),
            dma((chunks, sides, outer)), dma((chunks, sides, outer)),
            dma((chunks, lines)), dma((chunks, lines)),
        ],
        compiler_params=pltpu.CompilerParams(collective_id=1, has_side_effects=True),
    )(ids, weights, solved, basis, depth_mat, turn_mat)


def local(orbitals, pair_table, n_orb, n_slab):
    couples_own, slab_len, grid_len, width = orbitals.shape
    rows = slab_len * grid_len
    capacity = pair_table.shape[0]
    couples = couples_own * n_orb
    padded = jnp.pad(pair_table, ((0, 0), (0, 128 - pair_table.shape[1])), constant_values=-1)
    gathered, tables = gather_all(orbitals.reshape(couples_own * rows, width), padded, n_orb)
    gathered = gathered.reshape(couples, rows, width)
    table = tables.reshape(n_orb * capacity, 128)[:, :3]

    live_total = sum(capacity * (k + 1) // n_orb for k in range(n_orb))
    per_device = -(-live_total // n_orb)
    is_live = table[:, 0] >= 0
    rank = jnp.cumsum(is_live.astype(jnp.int32)) - 1
    wanted = jnp.arange(per_device, dtype=jnp.int32) * n_orb + lax.axis_index("orb")
    hits = (rank[None, :] == wanted[:, None]) & is_live[None, :]
    picked = jnp.sum(jnp.where(hits[:, :, None], table[None], 0), axis=1)
    used = jnp.any(hits, axis=1).astype(jnp.int32)
    ids = jnp.concatenate([picked, used[:, None]], axis=1)

    mat = hartley(grid_len)
    mat_high, mat_low = split_const(mat)
    turn_mat = jnp.asarray(np.concatenate([mat_high, mat_high, mat_low], axis=1))
    deep_high, deep_low = split_const(np.kron(np.eye(2, dtype=np.float32), mat))
    depth_mat = jnp.asarray(np.block([[deep_high, deep_low],
                                      [deep_high, np.zeros_like(deep_low)]]))
    kernel = coulomb(grid_len, slab_len, lax.axis_index("slab")).reshape(grid_len * slab_len, width)

    def whole(shape):
        return pl.BlockSpec(shape, lambda j, *ids: (0,) * len(shape))

    left_spec = pl.BlockSpec((1, rows, width), lambda j, ids: (ids[j, 0], 0, 0))
    right_spec = pl.BlockSpec((1, rows, width), lambda j, ids: (ids[j, 1], 0, 0))
    slot_spec = pl.BlockSpec((1, rows, width), lambda j, *ids: (j, 0, 0))
    slots_shape = jax.ShapeDtypeStruct((per_device, rows, width), jnp.float32)

    spectra = pl.pallas_call(
        functools.partial(forward_kernel, grid_len),
        out_shape=slots_shape,
        grid_spec=pltpu.PrefetchScalarGridSpec(
            num_scalar_prefetch=1, grid=(per_device,),
            in_specs=[left_spec, right_spec, whole(depth_mat.shape), whole(turn_mat.shape)],
            out_specs=slot_spec),
    )(ids, gathered, gathered, depth_mat, turn_mat)
    crossed = lax.all_to_all(spectra.reshape(per_device, slab_len, grid_len, width), "slab",
                             split_axis=2, concat_axis=1, tiled=True)
    solved = pl.pallas_call(
        functools.partial(middle_kernel, grid_len, slab_len),
        out_shape=slots_shape,
        grid=(per_device,),
        in_specs=[slot_spec, whole(kernel.shape), whole(turn_mat.shape)],
        out_specs=slot_spec,
    )(crossed.reshape(per_device, rows, width), kernel, turn_mat)
    couple_ids = jnp.arange(couples, dtype=jnp.int32)[:, None]
    first_on = (couple_ids == ids[None, :, 0]) & (ids[None, :, 3] == 1)
    second_on = (couple_ids == ids[None, :, 1]) & (ids[None, :, 3] == 1) & (
        ids[None, :, 0] != ids[None, :, 1])
    weights = jnp.stack([first_on, second_on], axis=2).reshape(couples, 2 * per_device)
    own = return_sum(ids, weights.astype(jnp.float32),
                     solved.reshape(per_device, grid_len, slab_len, width),
                     gathered, depth_mat, turn_mat, n_orb, n_slab)
    own = own.reshape(couples_own, rows, width)
    cell_count = grid_len * grid_len * grid_len

    def swap(values):
        return jnp.concatenate([values[..., grid_len:], values[..., :grid_len]], axis=-1)

    def lanes(values):
        summed = values.reshape(values.shape[:-1] + (2, grid_len)).sum(axis=-1)
        return jnp.repeat(summed, grid_len, axis=-1)

    basis = gathered.astype(jnp.float32)
    turned = swap(own)
    straight = jnp.sum(basis[None] * own[:, None], axis=2)
    across = jnp.sum(basis[None] * turned[:, None], axis=2)
    both = lax.psum(lanes(jnp.stack([straight, across])) / cell_count, "slab")
    kept = jnp.sum(both[0][:, :, None, :] * basis[None], axis=1)
    moved = jnp.sum(both[1][:, :, None, :] * basis[None], axis=1)
    return (own - kept - swap(moved)).reshape(orbitals.shape)


def solution(mesh):
    placed = (P("orb", "slab", None, None), P("orb", None))
    return jax.shard_map(
        functools.partial(local, n_orb=mesh.shape["orb"], n_slab=mesh.shape["slab"]),
        mesh=mesh, in_specs=placed, out_specs=P("orb", "slab", None, None), check_vma=False
    )
```

```python
import functools
import math

import jax
import jax.numpy as jnp
import numpy as np
from jax import lax
from jax.experimental import pallas as pl
from jax.experimental.pallas import tpu as pltpu
from jax.sharding import PartitionSpec as P

exchange_fraction = 0.25
cell_ratio = 8.0
MESH = pl.DeviceIdType.MESH
VMEM_SPEC = pl.BlockSpec(memory_space=pltpu.VMEM)
ANY_SPEC = pl.BlockSpec(memory_space=pl.ANY)


def folded(values, grid_len):
    return jnp.minimum(values, grid_len - values).astype(jnp.float32)


def hartley(grid_len):
    rows_idx = np.arange(grid_len)
    angles = 2.0 * math.pi / grid_len * (rows_idx[:, None] * rows_idx[None, :] % grid_len)
    return ((np.cos(angles) + np.sin(angles)) / math.sqrt(grid_len)).astype(np.float32)


def split_const(values):
    high = values.astype(jnp.bfloat16)
    return high, (values - high.astype(np.float32)).astype(jnp.bfloat16)


def split(values):
    high = values.astype(jnp.bfloat16)
    low = (values - high.astype(jnp.float32)).astype(jnp.bfloat16)
    return high, low


def coulomb(grid_len, slab_len, slab_index):
    planes_x = cell_ratio * folded(jnp.arange(grid_len, dtype=jnp.int32), grid_len)
    rows_y = folded(slab_index * slab_len + jnp.arange(slab_len, dtype=jnp.int32), grid_len)
    depth_z = folded(jnp.arange(2 * grid_len, dtype=jnp.int32) % grid_len, grid_len)
    scale_k = 2.0 * math.pi / grid_len * (2.0 * math.pi / grid_len)
    squared = scale_k * (
        planes_x[:, None, None] * planes_x[:, None, None]
        + rows_y[None, :, None] * rows_y[None, :, None]
        + depth_z[None, None, :] * depth_z[None, None, :]
    )
    safe_sq = jnp.where(squared > 0, squared, 1.0)
    return jnp.where(squared > 0, -exchange_fraction / safe_sq, 0.0)


def axis_parts(count):
    inner = 1
    while inner * inner * 4 <= count and count % (inner * 2) == 0:
        inner *= 2
    return count // inner, inner


def peer(index):
    return {"orb": index}


def greet_all(count, me):
    barrier = pltpu.get_barrier_semaphore()
    for step in range(1, count):
        pl.semaphore_signal(
            barrier, inc=1, device_id=peer(lax.rem(me + step, count)), device_id_type=MESH
        )
    pl.semaphore_wait(barrier, count - 1)


def table_kernel(count, table_ref, tables_ref, send_sem, recv_sem):
    me = lax.axis_index("orb")
    greet_all(count, me)

    def tab_copy(step):
        return pltpu.make_async_remote_copy(
            src_ref=table_ref, dst_ref=tables_ref.at[me], send_sem=send_sem.at[step - 1],
            recv_sem=recv_sem.at[step - 1], device_id=peer(lax.rem(me + step, count)),
            device_id_type=MESH)

    for step in range(1, count):
        tab_copy(step).start()
    tables_ref[me] = table_ref[...]
    for step in range(1, count):
        tab_copy(step).wait_recv()
    for step in range(1, count):
        tab_copy(step).wait_send()


def gather_tables(table, count):
    dma = pltpu.SemaphoreType.DMA
    return pl.pallas_call(
        functools.partial(table_kernel, count),
        out_shape=jax.ShapeDtypeStruct((count,) + table.shape, table.dtype),
        in_specs=[VMEM_SPEC],
        out_specs=VMEM_SPEC,
        scratch_shapes=[dma((count - 1,)), dma((count - 1,))],
        compiler_params=pltpu.CompilerParams(collective_id=0, has_side_effects=True),
    )(table)


def depth_turn(rows, depth_ref):
    width = rows.shape[1]
    high, low = split(rows)
    both = jnp.dot(jnp.concatenate([high, low], axis=1), depth_ref[...],
                   preferred_element_type=jnp.float32)
    return both[:, :width] + both[:, width:]


def pair_turn(first, second, left_ref):
    high, low = split(jnp.concatenate([first, second], axis=1))
    return jnp.dot(left_ref[...], jnp.concatenate([high, low, high], axis=0),
                   preferred_element_type=jnp.float32)


def greet_both(n_orb, n_slab, me, me_slab):
    barrier = pltpu.get_barrier_semaphore()
    for step in range(1, n_orb):
        pl.semaphore_signal(barrier, inc=1, device_id=peer(lax.rem(me + step, n_orb)),
                            device_id_type=MESH)
    for step in range(1, n_slab):
        pl.semaphore_signal(barrier, inc=1, device_id={"slab": lax.rem(me_slab + step, n_slab)},
                            device_id_type=MESH)
    pl.semaphore_wait(barrier, n_orb + n_slab - 2)


def chunk_count(slab_len):
    return max(1, min(4, slab_len // 2))


def advance_kernel(n_orb, n_slab, chunks, grid_len, ids_ref, own_ref, depth_ref, turn_ref,
                   basis_ref, out_ref, *scratch):
    held = scratch[:chunks]
    (spectra, keep_sem, stay_sem, up_send, up_recv, down_send, down_recv, side_send, side_recv,
     cross_send, cross_recv) = scratch[chunks:]
    outer, inner = axis_parts(n_orb)
    me, me_slab = lax.axis_index("orb"), lax.axis_index("slab")
    z_pos, x_pos = me // inner, me % inner
    couples_own = own_ref.shape[0]
    slots, _, slab_len, width = out_ref.shape
    planes = slab_len // chunks
    rows = planes * grid_len
    greet_both(n_orb, n_slab, me, me_slab)

    def mine(chunk):
        return own_ref.at[:, pl.ds(chunk * rows, rows)]

    def place(chunk, z_at):
        return held[chunk].at[pl.ds((z_at * inner + x_pos) * couples_own, couples_own)]

    def up_copy(chunk, step, src):
        return pltpu.make_async_remote_copy(
            src_ref=src, dst_ref=place(chunk, z_pos - step), send_sem=up_send.at[chunk, step],
            recv_sem=up_recv.at[chunk, step], device_id=peer((z_pos + 1) * inner + x_pos),
            device_id_type=MESH)

    def down_copy(chunk, step, src):
        return pltpu.make_async_remote_copy(
            src_ref=src, dst_ref=place(chunk, z_pos + step), send_sem=down_send.at[chunk, step],
            recv_sem=down_recv.at[chunk, step], device_id=peer((z_pos - 1) * inner + x_pos),
            device_id_type=MESH)

    def side_copy(chunk, hop, z_at, src):
        return pltpu.make_async_remote_copy(
            src_ref=src, dst_ref=place(chunk, z_at), send_sem=side_send.at[chunk, hop - 1, z_at],
            recv_sem=side_recv.at[chunk, hop - 1, z_at],
            device_id=peer(z_pos * inner + lax.rem(x_pos + hop, inner)), device_id_type=MESH)

    def keep_copy(chunk):
        return pltpu.make_async_copy(mine(chunk), place(chunk, z_pos), keep_sem.at[chunk])

    def cross_copy(chunk, hop):
        to = lax.rem(me_slab + hop, n_slab)
        return pltpu.make_async_remote_copy(
            src_ref=spectra.at[chunk, :, :,
                               pl.ds(pl.multiple_of(to * slab_len, slab_len), slab_len)],
            dst_ref=out_ref.at[:, pl.ds(me_slab * slab_len + chunk * planes, planes)],
            send_sem=cross_send.at[chunk, hop - 1], recv_sem=cross_recv.at[chunk, hop - 1],
            device_id={"slab": to}, device_id_type=MESH)

    def stay_copy(chunk):
        return pltpu.make_async_copy(
            spectra.at[chunk, :, :,
                       pl.ds(pl.multiple_of(me_slab * slab_len, slab_len), slab_len)],
            out_ref.at[:, pl.ds(me_slab * slab_len + chunk * planes, planes)],
            stay_sem.at[chunk])

    has_up, has_down = z_pos + 1 < outer, z_pos >= 1

    for chunk in range(chunks):
        @pl.when(has_up)
        def _():
            up_copy(chunk, 0, mine(chunk)).start()

        @pl.when(has_down)
        def _():
            down_copy(chunk, 0, mine(chunk)).start()

        for hop in range(1, inner):
            side_copy(chunk, hop, z_pos, mine(chunk)).start()
        keep_copy(chunk).start()

    def relay(chunk, step):
        @pl.when(z_pos - step >= 0)
        def _():
            got = place(chunk, z_pos - step)
            up_copy(chunk, step - 1, got).wait_recv()

            @pl.when(has_up)
            def _():
                up_copy(chunk, step, got).start()

            for hop in range(1, inner):
                side_copy(chunk, hop, z_pos - step, got).start()

        @pl.when(z_pos + step < outer)
        def _():
            got = place(chunk, z_pos + step)
            down_copy(chunk, step - 1, got).wait_recv()

            @pl.when(has_down)
            def _():
                down_copy(chunk, step, got).start()

            for hop in range(1, inner):
                side_copy(chunk, hop, z_pos + step, got).start()

    def compute(chunk):
        keep_copy(chunk).wait()
        for hop in range(1, inner):
            for z_at in range(outer):
                side_copy(chunk, hop, z_at, mine(chunk)).wait_recv()

        @pl.loop(0, slots)
        def _(slot):
            left = held[chunk][ids_ref[slot, 0]].astype(jnp.float32)
            right = held[chunk][ids_ref[slot, 1]].astype(jnp.float32)
            flipped = ids_ref[slot, 2] == 1
            partner = jnp.where(flipped, pltpu.roll(right, grid_len, 1), right)
            density = jnp.where(ids_ref[slot, 3] == 1, left * partner, 0.0)
            flat = depth_turn(density, depth_ref)
            for x_at in range(0, planes, 2):
                low, mid, high = x_at * grid_len, (x_at + 1) * grid_len, (x_at + 2) * grid_len
                done = pair_turn(flat[low:mid], flat[mid:high], turn_ref)
                spectra[chunk, slot, x_at] = done[:, :width]
                spectra[chunk, slot, x_at + 1] = done[:, width:]

        for hop in range(1, n_slab):
            cross_copy(chunk, hop).start()
        stay_copy(chunk).start()
        basis_ref[:, chunk * rows:(chunk + 1) * rows] = held[chunk][...]

    for wave in range(1, chunks + outer - 1):
        for step in range(outer - 1, 0, -1):
            if 0 <= wave - step < chunks:
                relay(wave - step, step)
        if wave - (outer - 1) >= 0:
            compute(wave - (outer - 1))

    for chunk in range(chunks):
        stay_copy(chunk).wait()
        for hop in range(1, n_slab):
            cross_copy(chunk, hop).wait_recv()
            cross_copy(chunk, hop).wait_send()
        for hop in range(1, inner):
            for z_at in range(outer):
                side_copy(chunk, hop, z_at, mine(chunk)).wait_send()
        for step in range(outer):
            @pl.when(has_up & (z_pos - step >= 0))
            def _():
                up_copy(chunk, step, mine(chunk)).wait_send()

            @pl.when(has_down & (z_pos + step < outer))
            def _():
                down_copy(chunk, step, mine(chunk)).wait_send()


def advance(ids, own, depth_mat, turn_mat, grid_len, n_orb, n_slab):
    outer, inner = axis_parts(n_orb)
    slots = ids.shape[0]
    couples_own, all_rows, width = own.shape
    slab_len = all_rows // grid_len
    chunks = chunk_count(slab_len)
    planes = slab_len // chunks
    rows = planes * grid_len
    sides, slabs = max(inner - 1, 1), max(n_slab - 1, 1)
    dma, vmem, f32 = pltpu.SemaphoreType.DMA, pltpu.VMEM, jnp.float32
    return pl.pallas_call(
        functools.partial(advance_kernel, n_orb, n_slab, chunks, grid_len),
        out_shape=(jax.ShapeDtypeStruct((n_orb * couples_own, all_rows, width), own.dtype),
                   jax.ShapeDtypeStruct((slots, grid_len, slab_len, width), f32)),
        in_specs=[pl.BlockSpec(memory_space=pltpu.SMEM)] + [VMEM_SPEC] * 3,
        out_specs=(VMEM_SPEC, VMEM_SPEC),
        scratch_shapes=[vmem((n_orb * couples_own, rows, width), own.dtype)] * chunks + [
            vmem((chunks, slots, planes, grid_len, width), f32),
            dma((chunks,)), dma((chunks,)),
            dma((chunks, outer)), dma((chunks, outer)), dma((chunks, outer)), dma((chunks, outer)),
            dma((chunks, sides, outer)), dma((chunks, sides, outer)),
            dma((chunks, slabs)), dma((chunks, slabs)),
        ],
        compiler_params=pltpu.CompilerParams(collective_id=2, has_side_effects=True),
    )(ids, own, depth_mat, turn_mat)


def middle_kernel(grid_len, slab_len, in_ref, kernel_ref, turn_ref, out_ref):
    width = in_ref.shape[2]
    for row in range(0, slab_len, 2):
        one = pl.ds(row, grid_len, stride=slab_len)
        two = pl.ds(row + 1, grid_len, stride=slab_len)
        done = pair_turn(in_ref[0, one, :], in_ref[0, two, :], turn_ref)
        back = pair_turn(done[:, :width] * kernel_ref[one, :], done[:, width:] * kernel_ref[two, :],
                         turn_ref)
        out_ref[0, one, :] = back[:, :width]
        out_ref[0, two, :] = back[:, width:]


def return_kernel(n_orb, n_slab, chunks, couples_own, ids_ref, weights_ref, solved_ref, basis_ref,
                  depth_ref, turn_ref, out_ref, back, terms, flat_ref, parts, side_in, line_in, sums,
                  keep_sem, back_send, back_recv, side_send, side_recv, line_send, line_recv):
    outer, inner = axis_parts(n_orb)
    me, me_slab = lax.axis_index("orb"), lax.axis_index("slab")
    z_pos, x_pos = me // inner, me % inner
    slots, grid_len, slab_len, width = solved_ref.shape
    planes = slab_len // chunks
    rows = planes * grid_len

    greet_both(n_orb, n_slab, me, me_slab)
    own_rows = pl.ds(pl.multiple_of(me_slab * slab_len, slab_len), slab_len)

    def back_copy(chunk, hop):
        to = lax.rem(me_slab + hop, n_slab)
        return pltpu.make_async_remote_copy(
            src_ref=solved_ref.at[:, pl.ds(to * slab_len + chunk * planes, planes)],
            dst_ref=back.at[chunk, :, :, own_rows],
            send_sem=back_send.at[chunk, hop - 1], recv_sem=back_recv.at[chunk, hop - 1],
            device_id={"slab": to}, device_id_type=MESH)

    def keep_copy(chunk):
        return pltpu.make_async_copy(
            solved_ref.at[:, pl.ds(me_slab * slab_len + chunk * planes, planes)],
            back.at[chunk, :, :, own_rows], keep_sem.at[chunk])

    def side_copy(chunk, hop, turn):
        z_at = lax.rem(z_pos + turn, outer)
        x_to = lax.rem(x_pos + hop, inner)
        return pltpu.make_async_remote_copy(
            src_ref=parts.at[chunk, z_at * inner + x_to], dst_ref=side_in.at[chunk, hop - 1, turn],
            send_sem=side_send.at[chunk, hop - 1, turn], recv_sem=side_recv.at[chunk, hop - 1, turn],
            device_id=peer(z_pos * inner + x_to), device_id_type=MESH)

    def line_copy(chunk, turn):
        z_at = lax.rem(z_pos + turn, outer)
        return pltpu.make_async_remote_copy(
            src_ref=sums.at[chunk, turn], dst_ref=line_in.at[chunk, turn - 1],
            send_sem=line_send.at[chunk, turn - 1], recv_sem=line_recv.at[chunk, turn - 1],
            device_id=peer(z_at * inner + x_pos), device_id_type=MESH)

    order = list(range(1, outer)) + [0]

    def compute(chunk):
        keep_copy(chunk).wait()
        for hop in range(1, n_slab):
            back_copy(chunk, hop).wait_recv()

        @pl.loop(0, slots)
        def _(slot):
            for x_at in range(0, planes, 2):
                done = pair_turn(back[chunk, slot, x_at], back[chunk, slot, x_at + 1], turn_ref)
                flat_ref[x_at * grid_len:(x_at + 1) * grid_len] = done[:, :width]
                flat_ref[(x_at + 1) * grid_len:(x_at + 2) * grid_len] = done[:, width:]
            potential = depth_turn(flat_ref[...], depth_ref)
            flipped = ids_ref[slot, 2] == 1
            span = pl.ds(chunk * rows, rows)
            right = basis_ref[ids_ref[slot, 1], span].astype(jnp.float32)
            left = basis_ref[ids_ref[slot, 0], span].astype(jnp.float32)
            terms[2 * slot] = potential * jnp.where(flipped, pltpu.roll(right, grid_len, 1), right)
            second = potential * left
            terms[2 * slot + 1] = jnp.where(flipped, pltpu.roll(second, grid_len, 1), second)

        tile = 32

        @pl.loop(0, rows // tile)
        def _(at):
            here = pl.ds(pl.multiple_of(at * tile, tile), tile)

            @pl.loop(0, n_orb)
            def _(owner):
                for k in range(couples_own):
                    total = jnp.zeros((tile, width), jnp.float32)
                    for term in range(2 * slots):
                        total += weights_ref[owner * couples_own + k, term] * terms[term, here]
                    parts[chunk, owner, k, here] = total

        for turn in order:
            for hop in range(1, inner):
                side_copy(chunk, hop, turn).start()

    def forward(chunk):
        for turn in order:
            merged = parts[chunk, lax.rem(z_pos + turn, outer) * inner + x_pos]
            for hop in range(1, inner):
                side_copy(chunk, hop, turn).wait_recv()
                merged = merged + side_in[chunk, hop - 1, turn]
            sums[chunk, turn] = merged
            if turn:
                line_copy(chunk, turn).start()

    for chunk in range(chunks):
        for hop in range(1, n_slab):
            back_copy(chunk, hop).start()
        keep_copy(chunk).start()
    for chunk in range(chunks):
        compute(chunk)
        if chunk:
            forward(chunk - 1)
    forward(chunks - 1)
    for chunk in range(chunks):
        total = sums[chunk, 0]
        for turn in range(1, outer):
            line_copy(chunk, turn).wait_recv()
            total = total + line_in[chunk, turn - 1]
        out_ref[:, chunk * rows:(chunk + 1) * rows] = total
    for chunk in range(chunks):
        for hop in range(1, n_slab):
            back_copy(chunk, hop).wait_send()
        for turn in range(outer):
            for hop in range(1, inner):
                side_copy(chunk, hop, turn).wait_send()
            if turn:
                line_copy(chunk, turn).wait_send()


def return_sum(ids, weights, solved, basis, depth_mat, turn_mat, n_orb, n_slab):
    outer, inner = axis_parts(n_orb)
    slots, grid_len, slab_len, width = solved.shape
    couples_own = basis.shape[0] // n_orb
    chunks = chunk_count(slab_len)
    planes = slab_len // chunks
    rows = planes * grid_len
    sides, lines = max(inner - 1, 1), max(outer - 1, 1)
    dma, vmem, f32 = pltpu.SemaphoreType.DMA, pltpu.VMEM, jnp.float32
    smem = pl.BlockSpec(memory_space=pltpu.SMEM)
    block = (couples_own, rows, width)
    return pl.pallas_call(
        functools.partial(return_kernel, n_orb, n_slab, chunks, couples_own),
        out_shape=jax.ShapeDtypeStruct((couples_own, slab_len * grid_len, width), f32),
        in_specs=[smem, smem] + [VMEM_SPEC] * 4,
        out_specs=VMEM_SPEC,
        scratch_shapes=[
            vmem((chunks, slots, planes, grid_len, width), f32),
            vmem((2 * slots, rows, width), f32),
            vmem((rows, width), f32),
            vmem((chunks, n_orb) + block, f32),
            vmem((chunks, sides, outer) + block, f32),
            vmem((chunks, lines) + block, f32),
            vmem((chunks, outer) + block, f32),
            dma((chunks,)),
            dma((chunks, max(n_slab - 1, 1))), dma((chunks, max(n_slab - 1, 1))),
            dma((chunks, sides, outer)), dma((chunks, sides, outer)),
            dma((chunks, lines)), dma((chunks, lines)),
        ],
        compiler_params=pltpu.CompilerParams(collective_id=1, has_side_effects=True),
    )(ids, weights, solved, basis, depth_mat, turn_mat)


def local(orbitals, pair_table, n_orb, n_slab):
    couples_own, slab_len, grid_len, width = orbitals.shape
    rows = slab_len * grid_len
    capacity = pair_table.shape[0]
    couples = couples_own * n_orb
    padded = jnp.pad(pair_table, ((0, 0), (0, 128 - pair_table.shape[1])), constant_values=-1)
    tables = gather_tables(padded, n_orb)
    table = tables.reshape(n_orb * capacity, 128)[:, :3]

    live_total = sum(capacity * (k + 1) // n_orb for k in range(n_orb))
    per_device = -(-live_total // n_orb)
    is_live = table[:, 0] >= 0
    rank = jnp.cumsum(is_live.astype(jnp.int32)) - 1
    wanted = jnp.arange(per_device, dtype=jnp.int32) * n_orb + lax.axis_index("orb")
    hits = (rank[None, :] == wanted[:, None]) & is_live[None, :]
    picked = jnp.sum(jnp.where(hits[:, :, None], table[None], 0), axis=1)
    used = jnp.any(hits, axis=1).astype(jnp.int32)
    ids = jnp.concatenate([picked, used[:, None]], axis=1)

    mat = hartley(grid_len)
    mat_high, mat_low = split_const(mat)
    turn_mat = jnp.asarray(np.concatenate([mat_high, mat_high, mat_low], axis=1))
    deep_high, deep_low = split_const(np.kron(np.eye(2, dtype=np.float32), mat))
    depth_mat = jnp.asarray(np.block([[deep_high, deep_low],
                                      [deep_high, np.zeros_like(deep_low)]]))
    kernel = coulomb(grid_len, slab_len, lax.axis_index("slab")).reshape(grid_len * slab_len, width)

    def whole(shape):
        return pl.BlockSpec(shape, lambda j, *ids: (0,) * len(shape))

    slot_spec = pl.BlockSpec((1, rows, width), lambda j, *ids: (j, 0, 0))
    slots_shape = jax.ShapeDtypeStruct((per_device, rows, width), jnp.float32)

    gathered, crossed = advance(ids, orbitals.reshape(couples_own, rows, width), depth_mat,
                                turn_mat, grid_len, n_orb, n_slab)
    solved = pl.pallas_call(
        functools.partial(middle_kernel, grid_len, slab_len),
        out_shape=slots_shape,
        grid=(per_device,),
        in_specs=[slot_spec, whole(kernel.shape), whole(turn_mat.shape)],
        out_specs=slot_spec,
    )(crossed.reshape(per_device, rows, width), kernel, turn_mat)
    couple_ids = jnp.arange(couples, dtype=jnp.int32)[:, None]
    first_on = (couple_ids == ids[None, :, 0]) & (ids[None, :, 3] == 1)
    second_on = (couple_ids == ids[None, :, 1]) & (ids[None, :, 3] == 1) & (
        ids[None, :, 0] != ids[None, :, 1])
    weights = jnp.stack([first_on, second_on], axis=2).reshape(couples, 2 * per_device)
    own = return_sum(ids, weights.astype(jnp.float32),
                     solved.reshape(per_device, grid_len, slab_len, width),
                     gathered, depth_mat, turn_mat, n_orb, n_slab)
    own = own.reshape(couples_own, rows, width)
    cell_count = grid_len * grid_len * grid_len

    def swap(values):
        return jnp.concatenate([values[..., grid_len:], values[..., :grid_len]], axis=-1)

    def lanes(values):
        summed = values.reshape(values.shape[:-1] + (2, grid_len)).sum(axis=-1)
        return jnp.repeat(summed, grid_len, axis=-1)

    basis = gathered.astype(jnp.float32)
    turned = swap(own)
    straight = jnp.sum(basis[None] * own[:, None], axis=2)
    across = jnp.sum(basis[None] * turned[:, None], axis=2)
    both = lax.psum(lanes(jnp.stack([straight, across])) / cell_count, "slab")
    kept = jnp.sum(both[0][:, :, None, :] * basis[None], axis=1)
    moved = jnp.sum(both[1][:, :, None, :] * basis[None], axis=1)
    return (own - kept - swap(moved)).reshape(orbitals.shape)


def solution(mesh):
    placed = (P("orb", "slab", None, None), P("orb", None))
    return jax.shard_map(
        functools.partial(local, n_orb=mesh.shape["orb"], n_slab=mesh.shape["slab"]),
        mesh=mesh, in_specs=placed, out_specs=P("orb", "slab", None, None), check_vma=False
    )
```
